1024 devices in a mesh: wide: 64 (over y_lo, z, core), narrow: 16 (over x, y_hi).
Axes of the slice: x: 4, y: 8 (y_hi: 4, y_lo: 2; y = y_hi * 2 + y_lo), z: 16, core: 2. Of those that a mesh axis runs over, the one named last changes fastest.
Arguments:
- state: float32 [2, 134217728], P(None, ('wide', 'narrow')), may hold values from -6 to 6
- gates: float32 [4, 2, 128, 128], replicated, may hold values from -0.375 to 0.375
- phase_index: int32 [3, 128], replicated, may hold values from 0 to 255
Outputs:
- final_state: float32 [2, 134217728], P(None, ('wide', 'narrow'))
The draws below stay inside these ranges and needn't reach their ends.
All inputs are finite; a program needn't handle non-finite values.
Results may differ from the reference program's by a relative error of at most 0.00007.
Values sent between devices are 32-bit elements; how exact they have to be, the bound alone decides.
No kernel may reach another device: no remote copies, remote signals or barrier semaphores. Data moves between devices by JAX's collectives and lax.ppermute only.
A program may use at most 32 MiB of HBM per device.

```python
import math
import jax
import jax.numpy as jnp
from jax import lax

GATE = 128
LAYERS = 4
AMPS = 134217728
N_WIDE = 64
N_NARROW = 16


def plant(drawn, stream_key, low, largest):
    extent = drawn.shape
    spot = [jax.random.randint(jax.random.fold_in(stream_key, axis), (), 0, extent[axis]) for axis in range(len(extent))]
    drawn = drawn.at[tuple(spot)].set(low)
    longest = extent.index(max(extent))
    spot[longest] = (spot[longest] + 1) % extent[longest]
    return drawn.at[tuple(spot)].set(largest)


def shard_levels(stream_key, dims, cuts, least, largest):
    factor_of = 1.0
    for axis_at, shards_of in cuts:
        heights = jax.random.uniform(jax.random.fold_in(jax.random.fold_in(stream_key, 6), axis_at), (shards_of,), jnp.float32, least / len(cuts), largest / len(cuts))
        factor_of = factor_of * jnp.repeat(jnp.exp(heights), dims[axis_at] // shards_of).reshape((-1,) + (1,) * (len(dims) - 1 - axis_at))
    return factor_of


def scatter_about(own_key, extent, width, reach, split=(), dtype=jnp.bfloat16):
    loudness = shard_levels(own_key, extent, split, -0.22, 0.18) if split else 1.0
    entries = jax.random.normal(own_key, extent, jnp.float32) * width * loudness
    return jnp.minimum(jnp.maximum(entries, -reach), reach).astype(dtype)


def setup_inputs(seed: int = 0) -> dict:
    key_list = jax.random.split(jax.random.key(seed), 4)
    state = scatter_about(key_list[0], (2, AMPS), 1.0, 6.0, ((1, 1024),), jnp.float32)
    gates = scatter_about(key_list[1], (LAYERS, 2, GATE, GATE), (2 * GATE) ** -0.5, 0.375, (), jnp.float32)
    phase_index = plant(jax.random.randint(key_list[2], (3, GATE), 0, 256), jax.random.fold_in(key_list[2], 1), 0, 255).astype(jnp.int32)
    return dict(state=state, gates=gates, phase_index=phase_index)


angle_step = 2.0 * math.pi / 256.0


def real_form(gate_re, gate_im):
    upper = jnp.stack([gate_re, -gate_im], axis=1)
    lower = jnp.stack([gate_im, gate_re], axis=1)
    return jnp.stack([upper, lower], axis=0)


def apply_last(blocks, amplitudes):
    return jnp.einsum("pmqn,qrn->prm", blocks, amplitudes, precision=lax.Precision.HIGHEST)


def apply_middle(blocks, amplitudes):
    return jnp.einsum("pmqn,qbnc->pbmc", blocks, amplitudes, precision=lax.Precision.HIGHEST)


def rotate(amplitudes, angle_sum):
    angles = angle_sum.astype(jnp.float32) * angle_step
    cosine = jnp.cos(angles)
    sine = jnp.sin(angles)
    real_part = amplitudes[0] * cosine - amplitudes[1] * sine
    imag_part = amplitudes[0] * sine + amplitudes[1] * cosine
    return jnp.stack([real_part, imag_part], axis=0)


def reference(state, gates, phase_index):
    row_count = AMPS // GATE
    local_amps = AMPS // (N_WIDE * N_NARROW)
    half_gate = GATE // 2
    amps = apply_last(real_form(gates[0, 0], gates[0, 1]), state.reshape(2, row_count, GATE))
    amps = apply_middle(real_form(gates[1, 0], gates[1, 1]), amps.reshape(2, AMPS // (GATE * GATE), GATE, GATE))
    row_ids = lax.iota(jnp.int32, row_count)
    middle_part = phase_index[1][row_ids % GATE]
    top_part = phase_index[2][row_ids // (AMPS // (GATE * GATE))]
    angle_sum = phase_index[0][None, :] + (middle_part + top_part)[:, None]
    amps = rotate(amps.reshape(2, row_count, GATE), angle_sum)
    moved = amps.reshape(2, N_WIDE, N_NARROW, N_NARROW, local_amps // N_NARROW).swapaxes(2, 3)
    moved = apply_middle(real_form(gates[2, 0], gates[2, 1]), moved.reshape(2, N_WIDE * N_NARROW, GATE, local_amps // GATE))
    blocks = real_form(gates[3, 0], gates[3, 1]).reshape(2, 2, half_gate, 2, 2, half_gate)
    grouped = moved.reshape(2, 2, N_WIDE * N_NARROW // 2, 2, half_gate, local_amps // GATE)
    moved = jnp.einsum("oxmiyn,iydtnr->oxdtmr", blocks, grouped, precision=lax.Precision.HIGHEST)
    back = moved.reshape(2, N_WIDE, N_NARROW, N_NARROW, local_amps // N_NARROW).swapaxes(2, 3)
    return back.reshape(2, AMPS)
```

```python
import math

import jax
import jax.numpy as jnp
from jax import lax
from jax.experimental import pallas as pl
from jax.experimental.pallas import tpu as pltpu
from jax.sharding import Mesh, PartitionSpec as P

GATE = 128
LANES = 128
GROUP = 32

angle_step = 2.0 * math.pi / 256.0


def dot(a, b):
    return jnp.dot(a, b, preferred_element_type=jnp.float32)


def split(value):
    high = value.astype(jnp.bfloat16)
    return high, (value - high.astype(jnp.float32)).astype(jnp.bfloat16)


def product(left, right):
    (left_high, left_low), (right_high, right_low) = left, right
    return dot(left_high, right_high) + (dot(left_high, right_low) + dot(left_low, right_high))


def real_form(gate_re, gate_im):
    upper = jnp.concatenate([gate_re, -gate_im], axis=1)
    lower = jnp.concatenate([gate_im, gate_re], axis=1)
    return jnp.concatenate([upper, lower], axis=0)


def first_kernel(x_ref, gates_ref, phase_ref, phase_smem, out_ref, phase_cols, mat_ref):
    top = lax.axis_index("top") * 64 + lax.axis_index("rest") * 2 + lax.axis_index("narrow") // 8
    top_phase = phase_smem[2, top]
    lane_angle = phase_ref[0:1, :].astype(jnp.float32) * angle_step
    row_angle = (phase_ref[1:2, :] + top_phase).astype(jnp.float32) * angle_step
    lane_cos, lane_sin = jnp.cos(lane_angle), jnp.sin(lane_angle)
    phase_cols[0] = jnp.broadcast_to(jnp.cos(row_angle), (GATE, LANES)).T
    phase_cols[1] = jnp.broadcast_to(jnp.sin(row_angle), (GATE, LANES)).T

    zero_re, zero_im = gates_ref[0, 0].T, gates_ref[0, 1].T
    turned_re = zero_re * lane_cos - zero_im * lane_sin
    turned_im = zero_re * lane_sin + zero_im * lane_cos
    right = split(
        jnp.concatenate(
            [
                jnp.concatenate([turned_re, turned_im], axis=1),
                jnp.concatenate([-turned_im, turned_re], axis=1),
            ],
            axis=0,
        )
    )
    for high in range(2):
        for low in range(8):
            rows = pl.ds(high * 64 + low, 8, stride=8)
            one_re, one_im = gates_ref[1, 0, rows, :], gates_ref[1, 1, rows, :]
            cosine, sine = phase_cols[0, rows, :], phase_cols[1, rows, :]
            turned_re = one_re * cosine - one_im * sine
            turned_im = one_re * sine + one_im * cosine
            at = high * 128 + low * 16
            mat_ref[at : at + 8, :LANES] = turned_re
            mat_ref[at : at + 8, LANES:] = -turned_im
            mat_ref[at + 8 : at + 16, :LANES] = turned_im
            mat_ref[at + 8 : at + 16, LANES:] = turned_re
    left = split(mat_ref[...])

    for pair in range(4):
        base = pair * 4 * GATE
        real = x_ref[pl.ds(base, 2 * GATE, stride=2), :]
        imag = x_ref[pl.ds(base + 1, 2 * GATE, stride=2), :]
        moved = product(split(jnp.concatenate([real, imag], axis=1)), right)
        turned = jnp.concatenate(
            [
                jnp.concatenate([moved[:GATE, :LANES], moved[GATE:, :LANES]], axis=1),
                jnp.concatenate([moved[:GATE, LANES:], moved[GATE:, LANES:]], axis=1),
            ],
            axis=0,
        )
        done = product(left, split(turned))
        for half in range(2):
            block = pair * 2 + half
            out_ref[block * 4 : block * 4 + 4] = done[:, half * LANES : (half + 1) * LANES].reshape(4, 64, LANES)


def second_kernel(x_ref, gates_ref, out_ref):
    third = split(real_form(gates_ref[2, 0], gates_ref[2, 1]))
    fourth = split(real_form(gates_ref[3, 0], gates_ref[3, 1]))
    for quarter in range(4):
        row = quarter * 16

        def part(which, side):
            rows = slice(row + side * 8, row + side * 8 + 8)
            return x_ref[which * 16 : which * 16 + 16, rows, :].reshape(GATE, LANES)

        gathered = jnp.concatenate(
            [jnp.concatenate([part(0, side), part(1, side)], axis=1) for side in range(2)], axis=0
        )
        moved = product(third, split(gathered))

        def piece(side, which, half):
            at = side * GATE + half * 64
            return moved[at : at + 64, which * LANES : (which + 1) * LANES]

        turned = jnp.concatenate(
            [
                jnp.concatenate([piece(side, which, 0), piece(side, which, 1)], axis=1)
                for side in range(2)
                for which in range(2)
            ],
            axis=0,
        )
        done = product(fourth, split(turned))
        for side in range(2):
            for which in range(2):
                for low in range(8):
                    for half in range(2):
                        at = side * 128 + which * 64 + low * 8
                        out_ref[which * 16 + half * 8 + low, pl.ds(quarter * 2 + side, 8, stride=8), :] = done[
                            at : at + 8, half * LANES : (half + 1) * LANES
                        ]


def last_kernel(x_ref, out_ref):
    for bit in range(2):
        out_ref[:, :, bit] = x_ref[:, bit]


def in_vmem():
    return pl.BlockSpec(memory_space=pltpu.VMEM)


def local(state, gates, phase_index):
    local_amps = state.shape[1]
    rows = state.reshape(2, local_amps // LANES, LANES).transpose(1, 0, 2).reshape(2 * local_amps // LANES, LANES)
    chunked = jax.ShapeDtypeStruct((GROUP, 64, LANES), jnp.float32)
    sent = pl.pallas_call(
        first_kernel,
        out_shape=chunked,
        in_specs=[in_vmem(), in_vmem(), in_vmem(), pl.BlockSpec(memory_space=pltpu.SMEM)],
        out_specs=in_vmem(),
        scratch_shapes=[
            pltpu.VMEM((2, GATE, LANES), jnp.float32),
            pltpu.VMEM((2 * GATE, 2 * GATE), jnp.float32),
        ],
    )(rows, gates, phase_index, phase_index)
    group = ("top", "narrow")
    held = lax.all_to_all(sent, group, 0, 0, tiled=True)
    back = pl.pallas_call(
        second_kernel,
        out_shape=chunked,
        in_specs=[in_vmem(), in_vmem()],
        out_specs=in_vmem(),
    )(held, gates)
    home = lax.all_to_all(back, group, 0, 0, tiled=True)
    ordered = pl.pallas_call(
        last_kernel,
        out_shape=jax.ShapeDtypeStruct((16, 8, 2, 8, LANES), jnp.float32),
        in_specs=[in_vmem()],
        out_specs=in_vmem(),
    )(home.reshape(16, 2, 8, 8, LANES))
    return ordered.reshape(local_amps // LANES, 2, LANES).transpose(1, 0, 2).reshape(2, local_amps)


def solution(mesh):
    wide, narrow = mesh.devices.shape
    split_mesh = Mesh(mesh.devices.reshape(2, wide // 2, narrow), ("top", "rest", "narrow"))
    amplitudes = P(None, ("top", "rest", "narrow"))
    return jax.shard_map(
        local, mesh=split_mesh, in_specs=(amplitudes, P(), P()), out_specs=amplitudes, check_vma=False
    )
```

```python
import math

import jax
import jax.numpy as jnp
from jax import lax
from jax.experimental import pallas as pl
from jax.experimental.pallas import tpu as pltpu
from jax.sharding import Mesh, PartitionSpec as P

GATE = 128
LANES = 128
STAGGER_NS = 14000
COPIES = 4
GROUP = 32
NARROW_BITS = ("n3", "n2", "n1", "n0")
ORDER = ("top", "n3", "n2", "n1", "n0")

angle_step = 2.0 * math.pi / 256.0


def place(top, narrow):
    bits = dict(zip(NARROW_BITS, (narrow >> 3, narrow >> 2 & 1, narrow >> 1 & 1, narrow & 1)), top=top)
    index = 0
    for name in ORDER:
        index = index * 2 + bits[name]
    return index


def dot(a, b):
    return jnp.dot(a, b, preferred_element_type=jnp.float32)


def split(value):
    high = value.astype(jnp.bfloat16)
    return high, (value - high.astype(jnp.float32)).astype(jnp.bfloat16)


def product(left, right):
    (left_high, left_low), (right_high, right_low) = left, right
    return dot(left_high, right_high) + (dot(left_high, right_low) + dot(left_low, right_high))


def real_form(gate_re, gate_im):
    upper = jnp.concatenate([gate_re, -gate_im], axis=1)
    lower = jnp.concatenate([gate_im, gate_re], axis=1)
    return jnp.concatenate([upper, lower], axis=0)


def first_kernel(
    state_ref, gates_hbm, phase_hbm, out_ref, later_ref, phase_ref, phase_cols, mat_ref, gates_ref, x_ref, sems, row_sems
):
    phase_copy = pltpu.make_async_copy(phase_hbm, phase_ref, sems.at[2])
    phase_copy.start()
    gate_copy = pltpu.make_async_copy(gates_hbm.at[0:2], gates_ref, sems.at[0])
    gate_copy.start()
    height = x_ref.shape[0] // COPIES
    row_copies = []
    for part in range(COPIES):
        rows = pl.ds(part * height, height)
        row_copies.append(pltpu.make_async_copy(state_ref.at[rows], x_ref.at[rows], row_sems.at[part]))
        row_copies[-1].start()
    later_copy = pltpu.make_async_copy(gates_hbm.at[2:4], later_ref, sems.at[1])
    later_copy.start()

    if STAGGER_NS:

        @pl.when(lax.axis_index("rest") % 2 == 1)
        def _():
            pl.delay(STAGGER_NS)

    top = lax.axis_index("top") * 64 + lax.axis_index("rest") * 2 + lax.axis_index("n3")
    phase_copy.wait()
    lane_ids = lax.broadcasted_iota(jnp.int32, (1, LANES), 1)
    top_phase = jnp.sum(jnp.where(lane_ids == top, phase_ref[2:3, :], 0), axis=1, keepdims=True)
    lane_angle = phase_ref[0:1, :].astype(jnp.float32) * angle_step
    row_angle = (phase_ref[1:2, :] + top_phase).astype(jnp.float32) * angle_step
    lane_cos, lane_sin = jnp.cos(lane_angle), jnp.sin(lane_angle)
    phase_cols[0] = jnp.broadcast_to(jnp.cos(row_angle), (GATE, LANES)).T
    phase_cols[1] = jnp.broadcast_to(jnp.sin(row_angle), (GATE, LANES)).T
    gate_copy.wait()

    zero_re, zero_im = gates_ref[0, 0].T, gates_ref[0, 1].T
    turned_re = zero_re * lane_cos - zero_im * lane_sin
    turned_im = zero_re * lane_sin + zero_im * lane_cos
    right = split(
        jnp.concatenate(
            [
                jnp.concatenate([turned_re, turned_im], axis=1),
                jnp.concatenate([-turned_im, turned_re], axis=1),
            ],
            axis=0,
        )
    )
    for high in range(2):
        for low in range(8):
            rows = pl.ds(high * 64 + low, 8, stride=8)
            one_re, one_im = gates_ref[1, 0, rows, :], gates_ref[1, 1, rows, :]
            cosine, sine = phase_cols[0, rows, :], phase_cols[1, rows, :]
            turned_re = one_re * cosine - one_im * sine
            turned_im = one_re * sine + one_im * cosine
            at = high * 128 + low * 16
            mat_ref[at : at + 8, :LANES] = turned_re
            mat_ref[at : at + 8, LANES:] = -turned_im
            mat_ref[at + 8 : at + 16, :LANES] = turned_im
            mat_ref[at + 8 : at + 16, LANES:] = turned_re
    left = split(mat_ref[...])
    for copy in row_copies:
        copy.wait()

    for pair in range(4):
        base = pair * 4 * GATE
        real = x_ref[pl.ds(base, 2 * GATE, stride=2), :]
        imag = x_ref[pl.ds(base + 1, 2 * GATE, stride=2), :]
        moved = product(split(jnp.concatenate([real, imag], axis=1)), right)
        turned = jnp.concatenate(
            [
                jnp.concatenate([moved[:GATE, :LANES], moved[GATE:, :LANES]], axis=1),
                jnp.concatenate([moved[:GATE, LANES:], moved[GATE:, LANES:]], axis=1),
            ],
            axis=0,
        )
        done = product(left, split(turned))
        for half in range(2):
            block = pair * 2 + half
            out_ref[block * 4 : block * 4 + 4] = done[:, half * LANES : (half + 1) * LANES].reshape(4, 64, LANES)
    later_copy.wait()


def second_kernel(x_ref, gates_ref, out_ref):
    third = split(real_form(gates_ref[0, 0], gates_ref[0, 1]))
    fourth = split(real_form(gates_ref[1, 0], gates_ref[1, 1]))
    for quarter in range(4):
        row = quarter * 16

        def part(which, side):
            rows = slice(row + side * 8, row + side * 8 + 8)
            return jnp.concatenate([x_ref[place(which, narrow), rows, :] for narrow in range(16)], axis=0)

        gathered = jnp.concatenate(
            [jnp.concatenate([part(0, side), part(1, side)], axis=1) for side in range(2)], axis=0
        )
        moved = product(third, split(gathered))

        def piece(side, which, half):
            at = side * GATE + half * 64
            return moved[at : at + 64, which * LANES : (which + 1) * LANES]

        turned = jnp.concatenate(
            [
                jnp.concatenate([piece(side, which, 0), piece(side, which, 1)], axis=1)
                for side in range(2)
                for which in range(2)
            ],
            axis=0,
        )
        done = product(fourth, split(turned))
        for side in range(2):
            for which in range(2):
                for low in range(8):
                    for half in range(2):
                        at = side * 128 + which * 64 + low * 8
                        out_ref[place(which, half * 8 + low), pl.ds(quarter * 2 + side, 8, stride=8), :] = done[
                            at : at + 8, half * LANES : (half + 1) * LANES
                        ]


def last_kernel(x_ref, out_ref, sems):
    copies = []
    for part in range(4):
        for bit in range(2):
            blocks = pl.ds(part * 4, 4)
            copies.append(
                pltpu.make_async_copy(x_ref.at[blocks, bit], out_ref.at[blocks, :, bit], sems.at[part * 2 + bit])
            )
            copies[-1].start()
    for copy in copies:
        copy.wait()


def in_vmem():
    return pl.BlockSpec(memory_space=pltpu.VMEM)


def anywhere():
    return pl.BlockSpec(memory_space=pl.ANY)


def exchange(chunks):
    return lax.all_to_all(chunks, ORDER, 0, 0, tiled=True)


def local(state, gates, phase_index):
    local_amps = state.shape[1]
    row_count = local_amps // LANES
    rows = state.reshape(2, row_count, LANES).transpose(1, 0, 2).reshape(2 * row_count, LANES)
    chunked = pltpu.VMEM((GROUP, 64, LANES), jnp.float32)
    half_gates = pltpu.VMEM((2, 2, GATE, GATE), jnp.float32)
    sent, later_gates = pl.pallas_call(
        first_kernel,
        out_shape=[chunked, half_gates],
        in_specs=[anywhere()] * 3,
        out_specs=[in_vmem(), in_vmem()],
        scratch_shapes=[
            pltpu.VMEM(phase_index.shape, jnp.int32),
            pltpu.VMEM((2, GATE, LANES), jnp.float32),
            pltpu.VMEM((2 * GATE, 2 * GATE), jnp.float32),
            half_gates,
            pltpu.VMEM((2 * row_count, LANES), jnp.float32),
            pltpu.SemaphoreType.DMA((3,)),
            pltpu.SemaphoreType.DMA((COPIES,)),
        ],
    )(rows, gates, phase_index)
    held = pltpu.with_memory_space_constraint(exchange(sent), pltpu.VMEM)
    back = pl.pallas_call(
        second_kernel,
        out_shape=chunked,
        in_specs=[in_vmem(), in_vmem()],
        out_specs=in_vmem(),
    )(held, pltpu.with_memory_space_constraint(later_gates, pltpu.VMEM))
    home = exchange(back).reshape(16, 2, 8, 8, LANES)
    ordered = pl.pallas_call(
        last_kernel,
        out_shape=jax.ShapeDtypeStruct((16, 8, 2, 8, LANES), jnp.float32),
        in_specs=[in_vmem()],
        out_specs=anywhere(),
        scratch_shapes=[pltpu.SemaphoreType.DMA((8,))],
    )(pltpu.with_memory_space_constraint(home, pltpu.VMEM))
    return ordered.reshape(row_count, 2, LANES).transpose(1, 0, 2).reshape(2, local_amps)


def solution(mesh):
    wide, narrow = mesh.devices.shape
    names = ("top", "rest") + NARROW_BITS
    split_mesh = Mesh(mesh.devices.reshape(2, wide // 2, *([2] * (narrow.bit_length() - 1))), names)
    amplitudes = P(None, names)
    return jax.shard_map(
        local, mesh=split_mesh, in_specs=(amplitudes, P(), P()), out_specs=amplitudes, check_vma=False
    )
```

```python
import math

import jax
import jax.numpy as jnp
from jax import lax
from jax.experimental import pallas as pl
from jax.experimental.pallas import tpu as pltpu
from jax.sharding import Mesh, PartitionSpec as P

GATE = 128
LANES = 128
STAGGER_NS = 14000
COPIES = 4
GROUP = 32
NARROW_BITS = ("n3", "n2", "n1", "n0")
ORDER = ("top", "n3", "n2", "n1", "n0")

angle_step = 2.0 * math.pi / 256.0


def place(top, narrow):
    bits = dict(zip(NARROW_BITS, (narrow >> 3, narrow >> 2 & 1, narrow >> 1 & 1, narrow & 1)), top=top)
    index = 0
    for name in ORDER:
        index = index * 2 + bits[name]
    return index


def dot(a, b):
    return jnp.dot(a, b, preferred_element_type=jnp.float32)


def split(value):
    high = value.astype(jnp.bfloat16)
    return high, (value - high.astype(jnp.float32)).astype(jnp.bfloat16)


def product(left, right):
    (left_high, left_low), (right_high, right_low) = left, right
    return dot(left_high, right_high) + (dot(left_high, right_low) + dot(left_low, right_high))


def real_form(gate_re, gate_im):
    upper = jnp.concatenate([gate_re, -gate_im], axis=1)
    lower = jnp.concatenate([gate_im, gate_re], axis=1)
    return jnp.concatenate([upper, lower], axis=0)


def first_kernel(
    state_ref, gates_hbm, phase_hbm, out_ref, later_ref, phase_ref, phase_cols, mat_ref, gates_ref, x_ref, sems, row_sems
):
    phase_copy = pltpu.make_async_copy(phase_hbm, phase_ref, sems.at[2])
    phase_copy.start()
    gate_copy = pltpu.make_async_copy(gates_hbm.at[0:2], gates_ref, sems.at[0])
    gate_copy.start()
    height = x_ref.shape[0] // COPIES
    row_copies = []
    for part in range(COPIES):
        rows = pl.ds(part * height, height)
        row_copies.append(pltpu.make_async_copy(state_ref.at[rows], x_ref.at[rows], row_sems.at[part]))
        row_copies[-1].start()
    later_copy = pltpu.make_async_copy(gates_hbm.at[2:4], later_ref, sems.at[1])
    later_copy.start()

    rest = lax.axis_index("rest")

    @pl.when((rest % 2 == 1) & (rest >= 2))
    def _():
        pl.delay(STAGGER_NS)

    top = lax.axis_index("top") * 64 + rest * 2 + lax.axis_index("n3")
    phase_copy.wait()
    lane_ids = lax.broadcasted_iota(jnp.int32, (1, LANES), 1)
    top_phase = jnp.sum(jnp.where(lane_ids == top, phase_ref[2:3, :], 0), axis=1, keepdims=True)
    lane_angle = phase_ref[0:1, :].astype(jnp.float32) * angle_step
    row_angle = (phase_ref[1:2, :] + top_phase).astype(jnp.float32) * angle_step
    lane_cos, lane_sin = jnp.cos(lane_angle), jnp.sin(lane_angle)
    phase_cols[0] = jnp.broadcast_to(jnp.cos(row_angle), (GATE, LANES)).T
    phase_cols[1] = jnp.broadcast_to(jnp.sin(row_angle), (GATE, LANES)).T
    gate_copy.wait()

    zero_re, zero_im = gates_ref[0, 0].T, gates_ref[0, 1].T
    turned_re = zero_re * lane_cos - zero_im * lane_sin
    turned_im = zero_re * lane_sin + zero_im * lane_cos
    right = split(
        jnp.concatenate(
            [
                jnp.concatenate([turned_re, turned_im], axis=1),
                jnp.concatenate([-turned_im, turned_re], axis=1),
            ],
            axis=0,
        )
    )
    for high in range(2):
        for low in range(8):
            rows = pl.ds(high * 64 + low, 8, stride=8)
            one_re, one_im = gates_ref[1, 0, rows, :], gates_ref[1, 1, rows, :]
            cosine, sine = phase_cols[0, rows, :], phase_cols[1, rows, :]
            turned_re = one_re * cosine - one_im * sine
            turned_im = one_re * sine + one_im * cosine
            at = high * 128 + low * 16
            mat_ref[at : at + 8, :LANES] = turned_re
            mat_ref[at : at + 8, LANES:] = -turned_im
            mat_ref[at + 8 : at + 16, :LANES] = turned_im
            mat_ref[at + 8 : at + 16, LANES:] = turned_re
    left = split(mat_ref[...])
    for copy in row_copies:
        copy.wait()

    for pair in range(4):
        base = pair * 4 * GATE
        real = x_ref[pl.ds(base, 2 * GATE, stride=2), :]
        imag = x_ref[pl.ds(base + 1, 2 * GATE, stride=2), :]
        moved = product(split(jnp.concatenate([real, imag], axis=1)), right)
        turned = jnp.concatenate(
            [
                jnp.concatenate([moved[:GATE, :LANES], moved[GATE:, :LANES]], axis=1),
                jnp.concatenate([moved[:GATE, LANES:], moved[GATE:, LANES:]], axis=1),
            ],
            axis=0,
        )
        done = product(left, split(turned))
        for half in range(2):
            block = pair * 2 + half
            out_ref[block * 4 : block * 4 + 4] = done[:, half * LANES : (half + 1) * LANES].reshape(4, 64, LANES)
    later_copy.wait()


def second_kernel(x_ref, gates_ref, out_ref):
    third = split(real_form(gates_ref[0, 0], gates_ref[0, 1]))
    fourth = split(real_form(gates_ref[1, 0], gates_ref[1, 1]))
    for quarter in range(4):
        row = quarter * 16

        def part(which, side):
            rows = slice(row + side * 8, row + side * 8 + 8)
            return jnp.concatenate([x_ref[place(which, narrow), rows, :] for narrow in range(16)], axis=0)

        gathered = jnp.concatenate(
            [jnp.concatenate([part(0, side), part(1, side)], axis=1) for side in range(2)], axis=0
        )
        moved = product(third, split(gathered))

        def piece(side, which, half):
            at = side * GATE + half * 64
            return moved[at : at + 64, which * LANES : (which + 1) * LANES]

        turned = jnp.concatenate(
            [
                jnp.concatenate([piece(side, which, 0), piece(side, which, 1)], axis=1)
                for side in range(2)
                for which in range(2)
            ],
            axis=0,
        )
        done = product(fourth, split(turned))
        for side in range(2):
            for which in range(2):
                for low in range(8):
                    for half in range(2):
                        at = side * 128 + which * 64 + low * 8
                        out_ref[place(which, half * 8 + low), pl.ds(quarter * 2 + side, 8, stride=8), :] = done[
                            at : at + 8, half * LANES : (half + 1) * LANES
                        ]


def last_kernel(x_ref, out_ref, sems):
    copies = []
    for part in range(4):
        for bit in range(2):
            blocks = pl.ds(part * 4, 4)
            copies.append(
                pltpu.make_async_copy(x_ref.at[blocks, bit], out_ref.at[blocks, :, bit], sems.at[part * 2 + bit])
            )
            copies[-1].start()
    for copy in copies:
        copy.wait()


def in_vmem():
    return pl.BlockSpec(memory_space=pltpu.VMEM)


def anywhere():
    return pl.BlockSpec(memory_space=pl.ANY)


def exchange(chunks):
    return lax.all_to_all(chunks, ORDER, 0, 0, tiled=True)


def local(state, gates, phase_index):
    local_amps = state.shape[1]
    row_count = local_amps // LANES
    rows = state.reshape(2, row_count, LANES).transpose(1, 0, 2).reshape(2 * row_count, LANES)
    chunked = pltpu.VMEM((GROUP, 64, LANES), jnp.float32)
    half_gates = pltpu.VMEM((2, 2, GATE, GATE), jnp.float32)
    sent, later_gates = pl.pallas_call(
        first_kernel,
        out_shape=[chunked, half_gates],
        in_specs=[anywhere()] * 3,
        out_specs=[in_vmem(), in_vmem()],
        scratch_shapes=[
            pltpu.VMEM(phase_index.shape, jnp.int32),
            pltpu.VMEM((2, GATE, LANES), jnp.float32),
            pltpu.VMEM((2 * GATE, 2 * GATE), jnp.float32),
            half_gates,
            pltpu.VMEM((2 * row_count, LANES), jnp.float32),
            pltpu.SemaphoreType.DMA((3,)),
            pltpu.SemaphoreType.DMA((COPIES,)),
        ],
    )(rows, gates, phase_index)
    held = pltpu.with_memory_space_constraint(exchange(sent), pltpu.VMEM)
    back = pl.pallas_call(
        second_kernel,
        out_shape=chunked,
        in_specs=[in_vmem(), in_vmem()],
        out_specs=in_vmem(),
    )(held, pltpu.with_memory_space_constraint(later_gates, pltpu.VMEM))
    home = exchange(back).reshape(16, 2, 8, 8, LANES)
    ordered = pl.pallas_call(
        last_kernel,
        out_shape=jax.ShapeDtypeStruct((16, 8, 2, 8, LANES), jnp.float32),
        in_specs=[in_vmem()],
        out_specs=anywhere(),
        scratch_shapes=[pltpu.SemaphoreType.DMA((8,))],
    )(pltpu.with_memory_space_constraint(home, pltpu.VMEM))
    return ordered.reshape(row_count, 2, LANES).transpose(1, 0, 2).reshape(2, local_amps)


def solution(mesh):
    wide, narrow = mesh.devices.shape
    names = ("top", "rest") + NARROW_BITS
    split_mesh = Mesh(mesh.devices.reshape(2, wide // 2, *([2] * (narrow.bit_length() - 1))), names)
    amplitudes = P(None, names)
    return jax.shard_map(
        local, mesh=split_mesh, in_specs=(amplitudes, P(), P()), out_specs=amplitudes, check_vma=False
    )
```

```python
import math

import jax
import jax.numpy as jnp
from jax import lax
from jax.experimental import pallas as pl
from jax.experimental.pallas import tpu as pltpu
from jax.sharding import Mesh, PartitionSpec as P

GATE = 128
LANES = 128
STAGGER_NS = 14000
FIRST_PLANE_NS = 3000
COPIES = 4
GROUP = 32
NARROW_BITS = ("n3", "n2", "n1", "n0")
ORDER = ("top", "n3", "n2", "n1", "n0")

angle_step = 2.0 * math.pi / 256.0


def place(top, narrow):
    bits = dict(zip(NARROW_BITS, (narrow >> 3, narrow >> 2 & 1, narrow >> 1 & 1, narrow & 1)), top=top)
    index = 0
    for name in ORDER:
        index = index * 2 + bits[name]
    return index


def dot(a, b):
    return jnp.dot(a, b, preferred_element_type=jnp.float32)


def split(value):
    high = value.astype(jnp.bfloat16)
    return high, (value - high.astype(jnp.float32)).astype(jnp.bfloat16)


def product(left, right):
    (left_high, left_low), (right_high, right_low) = left, right
    return dot(left_high, right_high) + (dot(left_high, right_low) + dot(left_low, right_high))


def real_form(gate_re, gate_im):
    upper = jnp.concatenate([gate_re, -gate_im], axis=1)
    lower = jnp.concatenate([gate_im, gate_re], axis=1)
    return jnp.concatenate([upper, lower], axis=0)


def first_kernel(
    state_ref, gates_hbm, phase_hbm, out_ref, later_ref, phase_ref, phase_cols, mat_ref, gates_ref, x_ref, sems, row_sems
):
    phase_copy = pltpu.make_async_copy(phase_hbm, phase_ref, sems.at[2])
    phase_copy.start()
    gate_copy = pltpu.make_async_copy(gates_hbm.at[0:2], gates_ref, sems.at[0])
    gate_copy.start()
    height = x_ref.shape[0] // COPIES
    row_copies = []
    for part in range(COPIES):
        rows = pl.ds(part * height, height)
        row_copies.append(pltpu.make_async_copy(state_ref.at[rows], x_ref.at[rows], row_sems.at[part]))
        row_copies[-1].start()
    later_copy = pltpu.make_async_copy(gates_hbm.at[2:4], later_ref, sems.at[1])
    later_copy.start()

    rest = lax.axis_index("rest")

    @pl.when((rest % 2 == 1) & (rest >= 2))
    def _():
        pl.delay(STAGGER_NS)

    @pl.when(rest == 0)
    def _():
        pl.delay(FIRST_PLANE_NS)

    top = lax.axis_index("top") * 64 + rest * 2 + lax.axis_index("n3")
    phase_copy.wait()
    lane_ids = lax.broadcasted_iota(jnp.int32, (1, LANES), 1)
    top_phase = jnp.sum(jnp.where(lane_ids == top, phase_ref[2:3, :], 0), axis=1, keepdims=True)
    lane_angle = phase_ref[0:1, :].astype(jnp.float32) * angle_step
    row_angle = (phase_ref[1:2, :] + top_phase).astype(jnp.float32) * angle_step
    lane_cos, lane_sin = jnp.cos(lane_angle), jnp.sin(lane_angle)
    phase_cols[0] = jnp.broadcast_to(jnp.cos(row_angle), (GATE, LANES)).T
    phase_cols[1] = jnp.broadcast_to(jnp.sin(row_angle), (GATE, LANES)).T
    gate_copy.wait()

    zero_re, zero_im = gates_ref[0, 0].T, gates_ref[0, 1].T
    turned_re = zero_re * lane_cos - zero_im * lane_sin
    turned_im = zero_re * lane_sin + zero_im * lane_cos
    right = split(
        jnp.concatenate(
            [
                jnp.concatenate([turned_re, turned_im], axis=1),
                jnp.concatenate([-turned_im, turned_re], axis=1),
            ],
            axis=0,
        )
    )
    for high in range(2):
        for low in range(8):
            rows = pl.ds(high * 64 + low, 8, stride=8)
            one_re, one_im = gates_ref[1, 0, rows, :], gates_ref[1, 1, rows, :]
            cosine, sine = phase_cols[0, rows, :], phase_cols[1, rows, :]
            turned_re = one_re * cosine - one_im * sine
            turned_im = one_re * sine + one_im * cosine
            at = high * 128 + low * 16
            mat_ref[at : at + 8, :LANES] = turned_re
            mat_ref[at : at + 8, LANES:] = -turned_im
            mat_ref[at + 8 : at + 16, :LANES] = turned_im
            mat_ref[at + 8 : at + 16, LANES:] = turned_re
    left = split(mat_ref[...])
    for copy in row_copies:
        copy.wait()

    for pair in range(4):
        base = pair * 4 * GATE
        real = x_ref[pl.ds(base, 2 * GATE, stride=2), :]
        imag = x_ref[pl.ds(base + 1, 2 * GATE, stride=2), :]
        moved = product(split(jnp.concatenate([real, imag], axis=1)), right)
        turned = jnp.concatenate(
            [
                jnp.concatenate([moved[:GATE, :LANES], moved[GATE:, :LANES]], axis=1),
                jnp.concatenate([moved[:GATE, LANES:], moved[GATE:, LANES:]], axis=1),
            ],
            axis=0,
        )
        done = product(left, split(turned))
        for half in range(2):
            block = pair * 2 + half
            out_ref[block * 4 : block * 4 + 4] = done[:, half * LANES : (half + 1) * LANES].reshape(4, 64, LANES)
    later_copy.wait()


def second_kernel(x_ref, gates_ref, out_ref):
    third = split(real_form(gates_ref[0, 0], gates_ref[0, 1]))
    fourth = split(real_form(gates_ref[1, 0], gates_ref[1, 1]))
    for quarter in range(4):
        row = quarter * 16

        def part(which, side):
            rows = slice(row + side * 8, row + side * 8 + 8)
            return jnp.concatenate([x_ref[place(which, narrow), rows, :] for narrow in range(16)], axis=0)

        gathered = jnp.concatenate(
            [jnp.concatenate([part(0, side), part(1, side)], axis=1) for side in range(2)], axis=0
        )
        moved = product(third, split(gathered))

        def piece(side, which, half):
            at = side * GATE + half * 64
            return moved[at : at + 64, which * LANES : (which + 1) * LANES]

        turned = jnp.concatenate(
            [
                jnp.concatenate([piece(side, which, 0), piece(side, which, 1)], axis=1)
                for side in range(2)
                for which in range(2)
            ],
            axis=0,
        )
        done = product(fourth, split(turned))
        for side in range(2):
            for which in range(2):
                for low in range(8):
                    for half in range(2):
                        at = side * 128 + which * 64 + low * 8
                        out_ref[place(which, half * 8 + low), pl.ds(quarter * 2 + side, 8, stride=8), :] = done[
                            at : at + 8, half * LANES : (half + 1) * LANES
                        ]


def last_kernel(x_ref, out_ref, sems):
    copies = []
    for part in range(4):
        for bit in range(2):
            blocks = pl.ds(part * 4, 4)
            copies.append(
                pltpu.make_async_copy(x_ref.at[blocks, bit], out_ref.at[blocks, :, bit], sems.at[part * 2 + bit])
            )
            copies[-1].start()
    for copy in copies:
        copy.wait()


def in_vmem():
    return pl.BlockSpec(memory_space=pltpu.VMEM)


def anywhere():
    return pl.BlockSpec(memory_space=pl.ANY)


def exchange(chunks):
    return lax.all_to_all(chunks, ORDER, 0, 0, tiled=True)


def local(state, gates, phase_index):
    local_amps = state.shape[1]
    row_count = local_amps // LANES
    rows = state.reshape(2, row_count, LANES).transpose(1, 0, 2).reshape(2 * row_count, LANES)
    chunked = pltpu.VMEM((GROUP, 64, LANES), jnp.float32)
    half_gates = pltpu.VMEM((2, 2, GATE, GATE), jnp.float32)
    sent, later_gates = pl.pallas_call(
        first_kernel,
        out_shape=[chunked, half_gates],
        in_specs=[anywhere()] * 3,
        out_specs=[in_vmem(), in_vmem()],
        scratch_shapes=[
            pltpu.VMEM(phase_index.shape, jnp.int32),
            pltpu.VMEM((2, GATE, LANES), jnp.float32),
            pltpu.VMEM((2 * GATE, 2 * GATE), jnp.float32),
            half_gates,
            pltpu.VMEM((2 * row_count, LANES), jnp.float32),
            pltpu.SemaphoreType.DMA((3,)),
            pltpu.SemaphoreType.DMA((COPIES,)),
        ],
    )(rows, gates, phase_index)
    held = pltpu.with_memory_space_constraint(exchange(sent), pltpu.VMEM)
    back = pl.pallas_call(
        second_kernel,
        out_shape=chunked,
        in_specs=[in_vmem(), in_vmem()],
        out_specs=in_vmem(),
    )(held, pltpu.with_memory_space_constraint(later_gates, pltpu.VMEM))
    home = exchange(back).reshape(16, 2, 8, 8, LANES)
    ordered = pl.pallas_call(
        last_kernel,
        out_shape=jax.ShapeDtypeStruct((16, 8, 2, 8, LANES), jnp.float32),
        in_specs=[in_vmem()],
        out_specs=anywhere(),
        scratch_shapes=[pltpu.SemaphoreType.DMA((8,))],
    )(pltpu.with_memory_space_constraint(home, pltpu.VMEM))
    return ordered.reshape(row_count, 2, LANES).transpose(1, 0, 2).reshape(2, local_amps)


def solution(mesh):
    wide, narrow = mesh.devices.shape
    names = ("top", "rest") + NARROW_BITS
    split_mesh = Mesh(mesh.devices.reshape(2, wide // 2, *([2] * (narrow.bit_length() - 1))), names)
    amplitudes = P(None, names)
    return jax.shard_map(
        local, mesh=split_mesh, in_specs=(amplitudes, P(), P()), out_specs=amplitudes, check_vma=False
    )
```

```python
import math

import jax
import jax.numpy as jnp
from jax import lax
from jax.experimental import pallas as pl
from jax.experimental.pallas import tpu as pltpu
from jax.sharding import Mesh, PartitionSpec as P

GATE = 128
LANES = 128
STAGGER_NS = 14000
FIRST_PLANE_NS = 4200
COPIES = 4
GROUP = 32
NARROW_BITS = ("n3", "n2", "n1", "n0")
ORDER = ("top", "n3", "n2", "n1", "n0")

angle_step = 2.0 * math.pi / 256.0


def place(top, narrow):
    bits = dict(zip(NARROW_BITS, (narrow >> 3, narrow >> 2 & 1, narrow >> 1 & 1, narrow & 1)), top=top)
    index = 0
    for name in ORDER:
        index = index * 2 + bits[name]
    return index


def dot(a, b):
    return jnp.dot(a, b, preferred_element_type=jnp.float32)


def split(value):
    high = value.astype(jnp.bfloat16)
    return high, (value - high.astype(jnp.float32)).astype(jnp.bfloat16)


def product(left, right):
    (left_high, left_low), (right_high, right_low) = left, right
    return dot(left_high, right_high) + (dot(left_high, right_low) + dot(left_low, right_high))


def real_form(gate_re, gate_im):
    upper = jnp.concatenate([gate_re, -gate_im], axis=1)
    lower = jnp.concatenate([gate_im, gate_re], axis=1)
    return jnp.concatenate([upper, lower], axis=0)


def first_kernel(
    state_ref, gates_hbm, phase_hbm, out_ref, later_ref, phase_ref, phase_cols, mat_ref, gates_ref, x_ref, sems, row_sems
):
    phase_copy = pltpu.make_async_copy(phase_hbm, phase_ref, sems.at[2])
    phase_copy.start()
    gate_copy = pltpu.make_async_copy(gates_hbm.at[0:2], gates_ref, sems.at[0])
    gate_copy.start()
    height = x_ref.shape[0] // COPIES
    row_copies = []
    for part in range(COPIES):
        rows = pl.ds(part * height, height)
        row_copies.append(pltpu.make_async_copy(state_ref.at[rows], x_ref.at[rows], row_sems.at[part]))
        row_copies[-1].start()
    later_copy = pltpu.make_async_copy(gates_hbm.at[2:4], later_ref, sems.at[1])
    later_copy.start()

    rest = lax.axis_index("rest")

    @pl.when((rest % 2 == 1) & (rest >= 2))
    def _():
        pl.delay(STAGGER_NS)

    @pl.when(rest == 0)
    def _():
        pl.delay(FIRST_PLANE_NS)

    top = lax.axis_index("top") * 64 + rest * 2 + lax.axis_index("n3")
    phase_copy.wait()
    lane_ids = lax.broadcasted_iota(jnp.int32, (1, LANES), 1)
    top_phase = jnp.sum(jnp.where(lane_ids == top, phase_ref[2:3, :], 0), axis=1, keepdims=True)
    lane_angle = phase_ref[0:1, :].astype(jnp.float32) * angle_step
    row_angle = (phase_ref[1:2, :] + top_phase).astype(jnp.float32) * angle_step
    lane_cos, lane_sin = jnp.cos(lane_angle), jnp.sin(lane_angle)
    phase_cols[0] = jnp.broadcast_to(jnp.cos(row_angle), (GATE, LANES)).T
    phase_cols[1] = jnp.broadcast_to(jnp.sin(row_angle), (GATE, LANES)).T
    gate_copy.wait()

    zero_re, zero_im = gates_ref[0, 0].T, gates_ref[0, 1].T
    turned_re = zero_re * lane_cos - zero_im * lane_sin
    turned_im = zero_re * lane_sin + zero_im * lane_cos
    right = split(
        jnp.concatenate(
            [
                jnp.concatenate([turned_re, turned_im], axis=1),
                jnp.concatenate([-turned_im, turned_re], axis=1),
            ],
            axis=0,
        )
    )
    for high in range(2):
        for low in range(8):
            rows = pl.ds(high * 64 + low, 8, stride=8)
            one_re, one_im = gates_ref[1, 0, rows, :], gates_ref[1, 1, rows, :]
            cosine, sine = phase_cols[0, rows, :], phase_cols[1, rows, :]
            turned_re = one_re * cosine - one_im * sine
            turned_im = one_re * sine + one_im * cosine
            at = high * 128 + low * 16
            mat_ref[at : at + 8, :LANES] = turned_re
            mat_ref[at : at + 8, LANES:] = -turned_im
            mat_ref[at + 8 : at + 16, :LANES] = turned_im
            mat_ref[at + 8 : at + 16, LANES:] = turned_re
    left = split(mat_ref[...])

    def stage_one(pair):
        base = pair * 4 * GATE
        real = x_ref[pl.ds(base, 2 * GATE, stride=2), :]
        imag = x_ref[pl.ds(base + 1, 2 * GATE, stride=2), :]
        return product(split(jnp.concatenate([real, imag], axis=1)), right)

    def stage_two(pair, moved):
        turned = jnp.concatenate(
            [
                jnp.concatenate([moved[:GATE, :LANES], moved[GATE:, :LANES]], axis=1),
                jnp.concatenate([moved[:GATE, LANES:], moved[GATE:, LANES:]], axis=1),
            ],
            axis=0,
        )
        done = product(left, split(turned))
        for half in range(2):
            block = pair * 2 + half
            out_ref[block * 4 : block * 4 + 4] = done[:, half * LANES : (half + 1) * LANES].reshape(4, 64, LANES)

    for copy in row_copies:
        copy.wait()
    moved = [stage_one(pair) for pair in range(4)]
    for pair in range(4):
        stage_two(pair, moved[pair])
    later_copy.wait()


def second_kernel(x_ref, gates_ref, out_ref):
    third = split(real_form(gates_ref[0, 0], gates_ref[0, 1]))
    fourth = split(real_form(gates_ref[1, 0], gates_ref[1, 1]))
    def stage_one(quarter):
        def part(which, side):
            rows = slice(quarter * 16 + side * 8, quarter * 16 + side * 8 + 8)
            return jnp.concatenate([x_ref[place(which, narrow), rows, :] for narrow in range(16)], axis=0)

        gathered = jnp.concatenate(
            [jnp.concatenate([part(0, side), part(1, side)], axis=1) for side in range(2)], axis=0
        )
        return product(third, split(gathered))

    def stage_two(quarter, moved):
        def piece(side, which, half):
            at = side * GATE + half * 64
            return moved[at : at + 64, which * LANES : (which + 1) * LANES]

        turned = jnp.concatenate(
            [
                jnp.concatenate([piece(side, which, 0), piece(side, which, 1)], axis=1)
                for side in range(2)
                for which in range(2)
            ],
            axis=0,
        )
        done = product(fourth, split(turned))
        for side in range(2):
            for which in range(2):
                for low in range(8):
                    for half in range(2):
                        at = side * 128 + which * 64 + low * 8
                        out_ref[place(which, half * 8 + low), pl.ds(quarter * 2 + side, 8, stride=8), :] = done[
                            at : at + 8, half * LANES : (half + 1) * LANES
                        ]

    moved = [stage_one(quarter) for quarter in range(4)]
    for quarter in range(4):
        stage_two(quarter, moved[quarter])


def last_kernel(x_ref, out_ref, sems):
    copies = []
    for part in range(4):
        for bit in range(2):
            blocks = pl.ds(part * 4, 4)
            copies.append(
                pltpu.make_async_copy(x_ref.at[blocks, bit], out_ref.at[blocks, :, bit], sems.at[part * 2 + bit])
            )
            copies[-1].start()
    for copy in copies:
        copy.wait()


def in_vmem():
    return pl.BlockSpec(memory_space=pltpu.VMEM)


def anywhere():
    return pl.BlockSpec(memory_space=pl.ANY)


def exchange(chunks):
    return lax.all_to_all(chunks, ORDER, 0, 0, tiled=True)


def local(state, gates, phase_index):
    local_amps = state.shape[1]
    row_count = local_amps // LANES
    rows = state.reshape(2, row_count, LANES).transpose(1, 0, 2).reshape(2 * row_count, LANES)
    chunked = pltpu.VMEM((GROUP, 64, LANES), jnp.float32)
    half_gates = pltpu.VMEM((2, 2, GATE, GATE), jnp.float32)
    sent, later_gates = pl.pallas_call(
        first_kernel,
        out_shape=[chunked, half_gates],
        in_specs=[anywhere()] * 3,
        out_specs=[in_vmem(), in_vmem()],
        scratch_shapes=[
            pltpu.VMEM(phase_index.shape, jnp.int32),
            pltpu.VMEM((2, GATE, LANES), jnp.float32),
            pltpu.VMEM((2 * GATE, 2 * GATE), jnp.float32),
            half_gates,
            pltpu.VMEM((2 * row_count, LANES), jnp.float32),
            pltpu.SemaphoreType.DMA((3,)),
            pltpu.SemaphoreType.DMA((COPIES,)),
        ],
    )(rows, gates, phase_index)
    held = pltpu.with_memory_space_constraint(exchange(sent), pltpu.VMEM)
    back = pl.pallas_call(
        second_kernel,
        out_shape=chunked,
        in_specs=[in_vmem(), in_vmem()],
        out_specs=in_vmem(),
    )(held, pltpu.with_memory_space_constraint(later_gates, pltpu.VMEM))
    home = exchange(back).reshape(16, 2, 8, 8, LANES)
    ordered = pl.pallas_call(
        last_kernel,
        out_shape=jax.ShapeDtypeStruct((16, 8, 2, 8, LANES), jnp.float32),
        in_specs=[in_vmem()],
        out_specs=anywhere(),
        scratch_shapes=[pltpu.SemaphoreType.DMA((8,))],
    )(pltpu.with_memory_space_constraint(home, pltpu.VMEM))
    return ordered.reshape(row_count, 2, LANES).transpose(1, 0, 2).reshape(2, local_amps)


def solution(mesh):
    wide, narrow = mesh.devices.shape
    names = ("top", "rest") + NARROW_BITS
    split_mesh = Mesh(mesh.devices.reshape(2, wide // 2, *([2] * (narrow.bit_length() - 1))), names)
    amplitudes = P(None, names)
    return jax.shard_map(
        local, mesh=split_mesh, in_specs=(amplitudes, P(), P()), out_specs=amplitudes, check_vma=False
    )
```

```python
import math

import jax
import jax.numpy as jnp
from jax import lax
from jax.experimental import pallas as pl
from jax.experimental.pallas import tpu as pltpu
from jax.sharding import Mesh, PartitionSpec as P

GATE = 128
LANES = 128
STAGGER_NS = 10800
FIRST_PLANE_NS = 4200
COPIES = 4
GROUP = 32
NARROW_BITS = ("n3", "n2", "n1", "n0")
ORDER = ("top", "n3", "n2", "n1", "n0")

angle_step = 2.0 * math.pi / 256.0


def place(top, narrow):
    bits = dict(zip(NARROW_BITS, (narrow >> 3, narrow >> 2 & 1, narrow >> 1 & 1, narrow & 1)), top=top)
    index = 0
    for name in ORDER:
        index = index * 2 + bits[name]
    return index


def dot(a, b):
    return jnp.dot(a, b, preferred_element_type=jnp.float32)


def split(value):
    high = value.astype(jnp.bfloat16)
    return high, (value - high.astype(jnp.float32)).astype(jnp.bfloat16)


def product(left, right):
    (left_high, left_low), (right_high, right_low) = left, right
    return dot(left_high, right_high) + (dot(left_high, right_low) + dot(left_low, right_high))


def real_form(gate_re, gate_im):
    upper = jnp.concatenate([gate_re, -gate_im], axis=1)
    lower = jnp.concatenate([gate_im, gate_re], axis=1)
    return jnp.concatenate([upper, lower], axis=0)


def first_kernel(
    state_ref, gates_hbm, phase_hbm, out_ref, later_ref, phase_ref, phase_cols, mat_ref, gates_ref, x_ref, sems, row_sems
):
    phase_copy = pltpu.make_async_copy(phase_hbm, phase_ref, sems.at[2])
    phase_copy.start()
    gate_copy = pltpu.make_async_copy(gates_hbm.at[0:2], gates_ref, sems.at[0])
    gate_copy.start()
    height = x_ref.shape[0] // COPIES
    row_copies = []
    for part in range(COPIES):
        rows = pl.ds(part * height, height)
        row_copies.append(pltpu.make_async_copy(state_ref.at[rows], x_ref.at[rows], row_sems.at[part]))
        row_copies[-1].start()
    later_copy = pltpu.make_async_copy(gates_hbm.at[2:4], later_ref, sems.at[1])
    later_copy.start()

    rest = lax.axis_index("rest")

    @pl.when((rest % 2 == 0) & (rest >= 2))
    def _():
        pl.delay(STAGGER_NS)

    @pl.when(rest == 0)
    def _():
        pl.delay(FIRST_PLANE_NS)

    top = lax.axis_index("top") * 64 + rest * 2 + lax.axis_index("n3")
    phase_copy.wait()
    lane_ids = lax.broadcasted_iota(jnp.int32, (1, LANES), 1)
    top_phase = jnp.sum(jnp.where(lane_ids == top, phase_ref[2:3, :], 0), axis=1, keepdims=True)
    lane_angle = phase_ref[0:1, :].astype(jnp.float32) * angle_step
    row_angle = (phase_ref[1:2, :] + top_phase).astype(jnp.float32) * angle_step
    lane_cos, lane_sin = jnp.cos(lane_angle), jnp.sin(lane_angle)
    phase_cols[0] = jnp.broadcast_to(jnp.cos(row_angle), (GATE, LANES)).T
    phase_cols[1] = jnp.broadcast_to(jnp.sin(row_angle), (GATE, LANES)).T
    gate_copy.wait()

    zero_re, zero_im = gates_ref[0, 0].T, gates_ref[0, 1].T
    turned_re = zero_re * lane_cos - zero_im * lane_sin
    turned_im = zero_re * lane_sin + zero_im * lane_cos
    right = split(
        jnp.concatenate(
            [
                jnp.concatenate([turned_re, turned_im], axis=1),
                jnp.concatenate([-turned_im, turned_re], axis=1),
            ],
            axis=0,
        )
    )
    for high in range(2):
        for low in range(8):
            rows = pl.ds(high * 64 + low, 8, stride=8)
            one_re, one_im = gates_ref[1, 0, rows, :], gates_ref[1, 1, rows, :]
            cosine, sine = phase_cols[0, rows, :], phase_cols[1, rows, :]
            turned_re = one_re * cosine - one_im * sine
            turned_im = one_re * sine + one_im * cosine
            at = high * 128 + low * 16
            mat_ref[at : at + 8, :LANES] = turned_re
            mat_ref[at : at + 8, LANES:] = -turned_im
            mat_ref[at + 8 : at + 16, :LANES] = turned_im
            mat_ref[at + 8 : at + 16, LANES:] = turned_re
    left = split(mat_ref[...])

    def stage_one(pair):
        base = pair * 4 * GATE
        real = x_ref[pl.ds(base, 2 * GATE, stride=2), :]
        imag = x_ref[pl.ds(base + 1, 2 * GATE, stride=2), :]
        return product(split(jnp.concatenate([real, imag], axis=1)), right)

    def stage_two(pair, moved):
        turned = jnp.concatenate(
            [
                jnp.concatenate([moved[:GATE, :LANES], moved[GATE:, :LANES]], axis=1),
                jnp.concatenate([moved[:GATE, LANES:], moved[GATE:, LANES:]], axis=1),
            ],
            axis=0,
        )
        done = product(left, split(turned))
        for half in range(2):
            block = pair * 2 + half
            out_ref[block * 4 : block * 4 + 4] = done[:, half * LANES : (half + 1) * LANES].reshape(4, 64, LANES)

    for copy in row_copies:
        copy.wait()
    moved = [stage_one(pair) for pair in range(4)]
    for pair in range(4):
        stage_two(pair, moved[pair])
    later_copy.wait()


def second_kernel(x_ref, gates_ref, out_ref):
    third = split(real_form(gates_ref[0, 0], gates_ref[0, 1]))
    fourth = split(real_form(gates_ref[1, 0], gates_ref[1, 1]))
    def stage_one(quarter):
        def part(which, side):
            rows = slice(quarter * 16 + side * 8, quarter * 16 + side * 8 + 8)
            return jnp.concatenate([x_ref[place(which, narrow), rows, :] for narrow in range(16)], axis=0)

        gathered = jnp.concatenate(
            [jnp.concatenate([part(0, side), part(1, side)], axis=1) for side in range(2)], axis=0
        )
        return product(third, split(gathered))

    def stage_two(quarter, moved):
        def piece(side, which, half):
            at = side * GATE + half * 64
            return moved[at : at + 64, which * LANES : (which + 1) * LANES]

        turned = jnp.concatenate(
            [
                jnp.concatenate([piece(side, which, 0), piece(side, which, 1)], axis=1)
                for side in range(2)
                for which in range(2)
            ],
            axis=0,
        )
        done = product(fourth, split(turned))
        for side in range(2):
            for which in range(2):
                for low in range(8):
                    for half in range(2):
                        at = side * 128 + which * 64 + low * 8
                        out_ref[place(which, half * 8 + low), pl.ds(quarter * 2 + side, 8, stride=8), :] = done[
                            at : at + 8, half * LANES : (half + 1) * LANES
                        ]

    moved = [stage_one(quarter) for quarter in range(4)]
    for quarter in range(4):
        stage_two(quarter, moved[quarter])


def last_kernel(x_ref, out_ref, sems):
    copies = []
    for part in range(4):
        for bit in range(2):
            blocks = pl.ds(part * 4, 4)
            copies.append(
                pltpu.make_async_copy(x_ref.at[blocks, bit], out_ref.at[blocks, :, bit], sems.at[part * 2 + bit])
            )
            copies[-1].start()
    for copy in copies:
        copy.wait()


def in_vmem():
    return pl.BlockSpec(memory_space=pltpu.VMEM)


def anywhere():
    return pl.BlockSpec(memory_space=pl.ANY)


def exchange(chunks):
    return lax.all_to_all(chunks, ORDER, 0, 0, tiled=True)


def local(state, gates, phase_index):
    local_amps = state.shape[1]
    row_count = local_amps // LANES
    rows = state.reshape(2, row_count, LANES).transpose(1, 0, 2).reshape(2 * row_count, LANES)
    chunked = pltpu.VMEM((GROUP, 64, LANES), jnp.float32)
    half_gates = pltpu.VMEM((2, 2, GATE, GATE), jnp.float32)
    sent, later_gates = pl.pallas_call(
        first_kernel,
        out_shape=[chunked, half_gates],
        in_specs=[anywhere()] * 3,
        out_specs=[in_vmem(), in_vmem()],
        scratch_shapes=[
            pltpu.VMEM(phase_index.shape, jnp.int32),
            pltpu.VMEM((2, GATE, LANES), jnp.float32),
            pltpu.VMEM((2 * GATE, 2 * GATE), jnp.float32),
            half_gates,
            pltpu.VMEM((2 * row_count, LANES), jnp.float32),
            pltpu.SemaphoreType.DMA((3,)),
            pltpu.SemaphoreType.DMA((COPIES,)),
        ],
    )(rows, gates, phase_index)
    held = pltpu.with_memory_space_constraint(exchange(sent), pltpu.VMEM)
    back = pl.pallas_call(
        second_kernel,
        out_shape=chunked,
        in_specs=[in_vmem(), in_vmem()],
        out_specs=in_vmem(),
    )(held, pltpu.with_memory_space_constraint(later_gates, pltpu.VMEM))
    home = exchange(back).reshape(16, 2, 8, 8, LANES)
    ordered = pl.pallas_call(
        last_kernel,
        out_shape=jax.ShapeDtypeStruct((16, 8, 2, 8, LANES), jnp.float32),
        in_specs=[in_vmem()],
        out_specs=anywhere(),
        scratch_shapes=[pltpu.SemaphoreType.DMA((8,))],
    )(pltpu.with_memory_space_constraint(home, pltpu.VMEM))
    return ordered.reshape(row_count, 2, LANES).transpose(1, 0, 2).reshape(2, local_amps)


def solution(mesh):
    wide, narrow = mesh.devices.shape
    names = ("top", "rest") + NARROW_BITS
    split_mesh = Mesh(mesh.devices.reshape(2, wide // 2, *([2] * (narrow.bit_length() - 1))), names)
    amplitudes = P(None, names)
    return jax.shard_map(
        local, mesh=split_mesh, in_specs=(amplitudes, P(), P()), out_specs=amplitudes, check_vma=False
    )
```

```python
import math

import jax
import jax.numpy as jnp
from jax import lax
from jax.experimental import pallas as pl
from jax.experimental.pallas import tpu as pltpu
from jax.sharding import Mesh, PartitionSpec as P

GATE = 128
LANES = 128
STAGGER_NS = 10400
FIRST_PLANE_NS = 3800
COPIES = 4
GROUP = 32
NARROW_BITS = ("n3", "n2", "n1", "n0")
ORDER = ("top", "n3", "n2", "n1", "n0")

angle_step = 2.0 * math.pi / 256.0


def place(top, narrow):
    bits = dict(zip(NARROW_BITS, (narrow >> 3, narrow >> 2 & 1, narrow >> 1 & 1, narrow & 1)), top=top)
    index = 0
    for name in ORDER:
        index = index * 2 + bits[name]
    return index


def dot(a, b):
    return jnp.dot(a, b, preferred_element_type=jnp.float32)


def split(value):
    high = value.astype(jnp.bfloat16)
    return high, (value - high.astype(jnp.float32)).astype(jnp.bfloat16)


def product(left, right):
    (left_high, left_low), (right_high, right_low) = left, right
    return dot(left_high, right_high) + (dot(left_high, right_low) + dot(left_low, right_high))


def real_form(gate_re, gate_im):
    upper = jnp.concatenate([gate_re, -gate_im], axis=1)
    lower = jnp.concatenate([gate_im, gate_re], axis=1)
    return jnp.concatenate([upper, lower], axis=0)


def blocks_swapped(value):
    return jnp.concatenate(
        [
            jnp.concatenate([value[:GATE, column : column + LANES], value[GATE:, column : column + LANES]], axis=1)
            for column in (0, LANES)
        ],
        axis=0,
    )


def first_kernel(
    state_ref, gates_hbm, phase_hbm, out_ref, later_ref, turn_ref, phase_ref, phase_cols, mat_ref, gates_ref, x_ref, sems, row_sems
):
    phase_copy = pltpu.make_async_copy(phase_hbm, phase_ref, sems.at[2])
    phase_copy.start()
    gate_copy = pltpu.make_async_copy(gates_hbm.at[0:2], gates_ref, sems.at[0])
    gate_copy.start()
    height = x_ref.shape[0] // COPIES
    row_copies = []
    for part in range(COPIES):
        rows = pl.ds(part * height, height)
        row_copies.append(pltpu.make_async_copy(state_ref.at[rows], x_ref.at[rows], row_sems.at[part]))
        row_copies[-1].start()
    later_copy = pltpu.make_async_copy(gates_hbm.at[2:4], later_ref, sems.at[1])
    later_copy.start()

    rest = lax.axis_index("rest")

    @pl.when((rest % 2 == 0) & (rest >= 2))
    def _():
        pl.delay(STAGGER_NS)

    @pl.when(rest == 0)
    def _():
        pl.delay(FIRST_PLANE_NS)

    top = lax.axis_index("top") * 64 + rest * 2 + lax.axis_index("n3")
    phase_copy.wait()
    lane_ids = lax.broadcasted_iota(jnp.int32, (1, LANES), 1)
    top_phase = jnp.sum(jnp.where(lane_ids == top, phase_ref[2:3, :], 0), axis=1, keepdims=True)
    lane_angle = phase_ref[0:1, :].astype(jnp.float32) * angle_step
    row_angle = (phase_ref[1:2, :] + top_phase).astype(jnp.float32) * angle_step
    lane_cos, lane_sin = jnp.cos(lane_angle), jnp.sin(lane_angle)
    phase_cols[0] = jnp.broadcast_to(jnp.cos(row_angle), (GATE, LANES)).T
    phase_cols[1] = jnp.broadcast_to(jnp.sin(row_angle), (GATE, LANES)).T
    gate_copy.wait()

    zero_re, zero_im = gates_ref[0, 0].T, gates_ref[0, 1].T
    turned_re = zero_re * lane_cos - zero_im * lane_sin
    turned_im = zero_re * lane_sin + zero_im * lane_cos
    turn_ref[...] = jnp.concatenate(
        [
            jnp.concatenate([turned_re, turned_im], axis=1),
            jnp.concatenate([-turned_im, turned_re], axis=1),
        ],
        axis=0,
    )
    for high in range(2):
        for low in range(8):
            rows = pl.ds(high * 64 + low, 8, stride=8)
            one_re, one_im = gates_ref[1, 0, rows, :], gates_ref[1, 1, rows, :]
            cosine, sine = phase_cols[0, rows, :], phase_cols[1, rows, :]
            turned_re = one_re * cosine - one_im * sine
            turned_im = one_re * sine + one_im * cosine
            at = high * 128 + low * 16
            mat_ref[at : at + 8, :LANES] = turned_re
            mat_ref[at : at + 8, LANES:] = -turned_im
            mat_ref[at + 8 : at + 16, :LANES] = turned_im
            mat_ref[at + 8 : at + 16, LANES:] = turned_re
    left = split(mat_ref[...])

    def rows_of(pair):
        base = pair * 4 * GATE
        return jnp.concatenate(
            [x_ref[pl.ds(base + part, 2 * GATE, stride=2), :] for part in range(2)], axis=1
        )

    def finish(pair, moved):
        done = product(left, split(blocks_swapped(moved)))
        for half in range(2):
            block = pair * 2 + half
            out_ref[block * 4 : block * 4 + 4] = done[:, half * LANES : (half + 1) * LANES].reshape(4, 64, LANES)

    for copy in row_copies:
        copy.wait()

    @pl.when(rest % 2 == 1)
    def _():
        for pair in range(4):
            finish(pair, rows_of(pair))

    @pl.when(rest % 2 == 0)
    def _():
        right = split(turn_ref[...])
        moved = [product(split(rows_of(pair)), right) for pair in range(4)]
        for pair in range(4):
            finish(pair, moved[pair])

    later_copy.wait()


def second_kernel(x_ref, gates_ref, turn_ref, out_ref):
    third = split(real_form(gates_ref[0, 0], gates_ref[0, 1]))
    fourth = split(real_form(gates_ref[1, 0], gates_ref[1, 1]))
    def gathered(quarter, by_part):
        def block(which, side):
            rows = slice(quarter * 16 + side * 8, quarter * 16 + side * 8 + 8)
            return jnp.concatenate([x_ref[place(which, narrow), rows, :] for narrow in range(16)], axis=0)

        return jnp.concatenate(
            [
                jnp.concatenate([block(other, outer) if by_part else block(outer, other) for other in range(2)], axis=1)
                for outer in range(2)
            ],
            axis=0,
        )

    def stage_two(quarter, moved):
        def piece(side, which, half):
            at = side * GATE + half * 64
            return moved[at : at + 64, which * LANES : (which + 1) * LANES]

        turned = jnp.concatenate(
            [
                jnp.concatenate([piece(side, which, 0), piece(side, which, 1)], axis=1)
                for side in range(2)
                for which in range(2)
            ],
            axis=0,
        )
        done = product(fourth, split(turned))
        for side in range(2):
            for which in range(2):
                for low in range(8):
                    for half in range(2):
                        at = side * 128 + which * 64 + low * 8
                        out_ref[place(which, half * 8 + low), pl.ds(quarter * 2 + side, 8, stride=8), :] = done[
                            at : at + 8, half * LANES : (half + 1) * LANES
                        ]

    rest = lax.axis_index("rest")

    @pl.when(rest % 2 == 1)
    def _():
        right = split(turn_ref[...])
        turned = [product(split(gathered(quarter, False)), right) for quarter in range(4)]
        moved = [product(third, split(blocks_swapped(turned[quarter]))) for quarter in range(4)]
        for quarter in range(4):
            stage_two(quarter, moved[quarter])

    @pl.when(rest % 2 == 0)
    def _():
        moved = [product(third, split(gathered(quarter, True))) for quarter in range(4)]
        for quarter in range(4):
            stage_two(quarter, moved[quarter])


def last_kernel(x_ref, out_ref, sems):
    copies = []
    for part in range(4):
        for bit in range(2):
            blocks = pl.ds(part * 4, 4)
            copies.append(
                pltpu.make_async_copy(x_ref.at[blocks, bit], out_ref.at[blocks, :, bit], sems.at[part * 2 + bit])
            )
            copies[-1].start()
    for copy in copies:
        copy.wait()


def in_vmem():
    return pl.BlockSpec(memory_space=pltpu.VMEM)


def anywhere():
    return pl.BlockSpec(memory_space=pl.ANY)


def exchange(chunks):
    return lax.all_to_all(chunks, ORDER, 0, 0, tiled=True)


def local(state, gates, phase_index):
    local_amps = state.shape[1]
    row_count = local_amps // LANES
    rows = state.reshape(2, row_count, LANES).transpose(1, 0, 2).reshape(2 * row_count, LANES)
    chunked = pltpu.VMEM((GROUP, 64, LANES), jnp.float32)
    half_gates = pltpu.VMEM((2, 2, GATE, GATE), jnp.float32)
    turn = pltpu.VMEM((2 * GATE, 2 * GATE), jnp.float32)
    sent, later_gates, lane_gate = pl.pallas_call(
        first_kernel,
        out_shape=[chunked, half_gates, turn],
        in_specs=[anywhere()] * 3,
        out_specs=[in_vmem()] * 3,
        scratch_shapes=[
            pltpu.VMEM(phase_index.shape, jnp.int32),
            pltpu.VMEM((2, GATE, LANES), jnp.float32),
            pltpu.VMEM((2 * GATE, 2 * GATE), jnp.float32),
            half_gates,
            pltpu.VMEM((2 * row_count, LANES), jnp.float32),
            pltpu.SemaphoreType.DMA((3,)),
            pltpu.SemaphoreType.DMA((COPIES,)),
        ],
    )(rows, gates, phase_index)
    held = pltpu.with_memory_space_constraint(exchange(sent), pltpu.VMEM)
    back = pl.pallas_call(
        second_kernel,
        out_shape=chunked,
        in_specs=[in_vmem()] * 3,
        out_specs=in_vmem(),
    )(
        held,
        pltpu.with_memory_space_constraint(later_gates, pltpu.VMEM),
        pltpu.with_memory_space_constraint(lane_gate, pltpu.VMEM),
    )
    home = exchange(back).reshape(16, 2, 8, 8, LANES)
    ordered = pl.pallas_call(
        last_kernel,
        out_shape=jax.ShapeDtypeStruct((16, 8, 2, 8, LANES), jnp.float32),
        in_specs=[in_vmem()],
        out_specs=anywhere(),
        scratch_shapes=[pltpu.SemaphoreType.DMA((8,))],
    )(pltpu.with_memory_space_constraint(home, pltpu.VMEM))
    return ordered.reshape(row_count, 2, LANES).transpose(1, 0, 2).reshape(2, local_amps)


def solution(mesh):
    wide, narrow = mesh.devices.shape
    names = ("top", "rest") + NARROW_BITS
    split_mesh = Mesh(mesh.devices.reshape(2, wide // 2, *([2] * (narrow.bit_length() - 1))), names)
    amplitudes = P(None, names)
    return jax.shard_map(
        local, mesh=split_mesh, in_specs=(amplitudes, P(), P()), out_specs=amplitudes, check_vma=False
    )
```

```python
import math

import jax
import jax.numpy as jnp
from jax import lax
from jax.experimental import pallas as pl
from jax.experimental.pallas import tpu as pltpu
from jax.sharding import Mesh, PartitionSpec as P

GATE = 128
LANES = 128
STAGGER_NS = 10200
FIRST_PLANE_NS = 3300
COPIES = 4
GROUP = 32
NARROW_BITS = ("n3", "n2", "n1", "n0")
ORDER = ("top", "n3", "n2", "n1", "n0")

angle_step = 2.0 * math.pi / 256.0


def place(top, narrow):
    bits = dict(zip(NARROW_BITS, (narrow >> 3, narrow >> 2 & 1, narrow >> 1 & 1, narrow & 1)), top=top)
    index = 0
    for name in ORDER:
        index = index * 2 + bits[name]
    return index


def dot(a, b):
    return jnp.dot(a, b, preferred_element_type=jnp.float32)


def split(value):
    high = value.astype(jnp.bfloat16)
    return high, (value - high.astype(jnp.float32)).astype(jnp.bfloat16)


def product(left, right):
    (left_high, left_low), (right_high, right_low) = left, right
    return dot(left_high, right_high) + (dot(left_high, right_low) + dot(left_low, right_high))


def real_form(gate_re, gate_im):
    upper = jnp.concatenate([gate_re, -gate_im], axis=1)
    lower = jnp.concatenate([gate_im, gate_re], axis=1)
    return jnp.concatenate([upper, lower], axis=0)


def blocks_swapped(value):
    return jnp.concatenate(
        [
            jnp.concatenate([value[:GATE, column : column + LANES], value[GATE:, column : column + LANES]], axis=1)
            for column in (0, LANES)
        ],
        axis=0,
    )


def first_kernel(
    state_ref, gates_hbm, phase_hbm, out_ref, later_ref, turn_ref, ready_ref, phase_ref, phase_cols, mat_ref, gates_ref, x_ref,
    sems, row_sems
):
    phase_copy = pltpu.make_async_copy(phase_hbm, phase_ref, sems.at[2])
    phase_copy.start()
    gate_copy = pltpu.make_async_copy(gates_hbm.at[0:2], gates_ref, sems.at[0])
    gate_copy.start()
    height = x_ref.shape[0] // COPIES
    row_copies = []
    for part in range(COPIES):
        rows = pl.ds(part * height, height)
        row_copies.append(pltpu.make_async_copy(state_ref.at[rows], x_ref.at[rows], row_sems.at[part]))
        row_copies[-1].start()
    later_copy = pltpu.make_async_copy(gates_hbm.at[2:4], later_ref, sems.at[1])
    later_copy.start()

    rest = lax.axis_index("rest")

    @pl.when((rest % 2 == 0) & (rest >= 2))
    def _():
        pl.delay(STAGGER_NS)

    @pl.when(rest == 0)
    def _():
        pl.delay(FIRST_PLANE_NS)

    top = lax.axis_index("top") * 64 + rest * 2 + lax.axis_index("n3")
    phase_copy.wait()
    lane_ids = lax.broadcasted_iota(jnp.int32, (1, LANES), 1)
    top_phase = jnp.sum(jnp.where(lane_ids == top, phase_ref[2:3, :], 0), axis=1, keepdims=True)
    lane_angle = phase_ref[0:1, :].astype(jnp.float32) * angle_step
    row_angle = (phase_ref[1:2, :] + top_phase).astype(jnp.float32) * angle_step
    lane_cos, lane_sin = jnp.cos(lane_angle), jnp.sin(lane_angle)
    phase_cols[0] = jnp.broadcast_to(jnp.cos(row_angle), (GATE, LANES)).T
    phase_cols[1] = jnp.broadcast_to(jnp.sin(row_angle), (GATE, LANES)).T
    gate_copy.wait()

    zero_re, zero_im = gates_ref[0, 0].T, gates_ref[0, 1].T
    turned_re = zero_re * lane_cos - zero_im * lane_sin
    turned_im = zero_re * lane_sin + zero_im * lane_cos
    turn_ref[...] = jnp.concatenate(
        [
            jnp.concatenate([turned_re, turned_im], axis=1),
            jnp.concatenate([-turned_im, turned_re], axis=1),
        ],
        axis=0,
    )
    for high in range(2):
        for low in range(8):
            rows = pl.ds(high * 64 + low, 8, stride=8)
            one_re, one_im = gates_ref[1, 0, rows, :], gates_ref[1, 1, rows, :]
            cosine, sine = phase_cols[0, rows, :], phase_cols[1, rows, :]
            turned_re = one_re * cosine - one_im * sine
            turned_im = one_re * sine + one_im * cosine
            at = high * 128 + low * 16
            mat_ref[at : at + 8, :LANES] = turned_re
            mat_ref[at : at + 8, LANES:] = -turned_im
            mat_ref[at + 8 : at + 16, :LANES] = turned_im
            mat_ref[at + 8 : at + 16, LANES:] = turned_re
    left = split(mat_ref[...])

    def rows_of(pair):
        base = pair * 4 * GATE
        return jnp.concatenate(
            [x_ref[pl.ds(base + part, 2 * GATE, stride=2), :] for part in range(2)], axis=1
        )

    def finish(pair, moved):
        done = product(left, split(blocks_swapped(moved)))
        for half in range(2):
            block = pair * 2 + half
            out_ref[block * 4 : block * 4 + 4] = done[:, half * LANES : (half + 1) * LANES].reshape(4, 64, LANES)

    for copy in row_copies:
        copy.wait()

    @pl.when(rest % 2 == 1)
    def _():
        for pair in range(4):
            finish(pair, rows_of(pair))
        later_copy.wait()

    @pl.when(rest % 2 == 0)
    def _():
        later_copy.wait()
        for gate in range(2):
            ready_ref[gate, 0], ready_ref[gate, 1] = split(real_form(later_ref[gate, 0], later_ref[gate, 1]))
        right = split(turn_ref[...])
        moved = [product(split(rows_of(pair)), right) for pair in range(4)]
        for pair in range(4):
            finish(pair, moved[pair])


def second_kernel(x_ref, gates_ref, turn_ref, ready_ref, out_ref):
    def gathered(quarter, by_part):
        def block(which, side):
            rows = slice(quarter * 16 + side * 8, quarter * 16 + side * 8 + 8)
            return jnp.concatenate([x_ref[place(which, narrow), rows, :] for narrow in range(16)], axis=0)

        return jnp.concatenate(
            [
                jnp.concatenate([block(other, outer) if by_part else block(outer, other) for other in range(2)], axis=1)
                for outer in range(2)
            ],
            axis=0,
        )

    def stage_two(quarter, moved, fourth):
        def piece(side, which, half):
            at = side * GATE + half * 64
            return moved[at : at + 64, which * LANES : (which + 1) * LANES]

        turned = jnp.concatenate(
            [
                jnp.concatenate([piece(side, which, 0), piece(side, which, 1)], axis=1)
                for side in range(2)
                for which in range(2)
            ],
            axis=0,
        )
        done = product(fourth, split(turned))
        for side in range(2):
            for which in range(2):
                for low in range(8):
                    for half in range(2):
                        at = side * 128 + which * 64 + low * 8
                        out_ref[place(which, half * 8 + low), pl.ds(quarter * 2 + side, 8, stride=8), :] = done[
                            at : at + 8, half * LANES : (half + 1) * LANES
                        ]

    rest = lax.axis_index("rest")

    @pl.when(rest % 2 == 1)
    def _():
        third, fourth = (split(real_form(gates_ref[gate, 0], gates_ref[gate, 1])) for gate in range(2))
        right = split(turn_ref[...])
        turned = [product(split(gathered(quarter, False)), right) for quarter in range(4)]
        moved = [product(third, split(blocks_swapped(turned[quarter]))) for quarter in range(4)]
        for quarter in range(4):
            stage_two(quarter, moved[quarter], fourth)

    @pl.when(rest % 2 == 0)
    def _():
        third, fourth = ((ready_ref[gate, 0], ready_ref[gate, 1]) for gate in range(2))
        moved = [product(third, split(gathered(quarter, True))) for quarter in range(4)]
        for quarter in range(4):
            stage_two(quarter, moved[quarter], fourth)


def last_kernel(x_ref, out_ref, sems):
    copies = []
    for part in range(4):
        for bit in range(2):
            blocks = pl.ds(part * 4, 4)
            copies.append(
                pltpu.make_async_copy(x_ref.at[blocks, bit], out_ref.at[blocks, :, bit], sems.at[part * 2 + bit])
            )
            copies[-1].start()
    for copy in copies:
        copy.wait()


def in_vmem():
    return pl.BlockSpec(memory_space=pltpu.VMEM)


def anywhere():
    return pl.BlockSpec(memory_space=pl.ANY)


def exchange(chunks):
    return lax.all_to_all(chunks, ORDER, 0, 0, tiled=True)


def local(state, gates, phase_index):
    local_amps = state.shape[1]
    row_count = local_amps // LANES
    rows = state.reshape(2, row_count, LANES).transpose(1, 0, 2).reshape(2 * row_count, LANES)
    chunked = pltpu.VMEM((GROUP, 64, LANES), jnp.float32)
    half_gates = pltpu.VMEM((2, 2, GATE, GATE), jnp.float32)
    turn = pltpu.VMEM((2 * GATE, 2 * GATE), jnp.float32)
    ready = pltpu.VMEM((2, 2, 2 * GATE, 2 * GATE), jnp.bfloat16)
    sent, later_gates, lane_gate, ready_gates = pl.pallas_call(
        first_kernel,
        out_shape=[chunked, half_gates, turn, ready],
        in_specs=[anywhere()] * 3,
        out_specs=[in_vmem()] * 4,
        scratch_shapes=[
            pltpu.VMEM(phase_index.shape, jnp.int32),
            pltpu.VMEM((2, GATE, LANES), jnp.float32),
            pltpu.VMEM((2 * GATE, 2 * GATE), jnp.float32),
            half_gates,
            pltpu.VMEM((2 * row_count, LANES), jnp.float32),
            pltpu.SemaphoreType.DMA((3,)),
            pltpu.SemaphoreType.DMA((COPIES,)),
        ],
    )(rows, gates, phase_index)
    held = pltpu.with_memory_space_constraint(exchange(sent), pltpu.VMEM)
    back = pl.pallas_call(
        second_kernel,
        out_shape=chunked,
        in_specs=[in_vmem()] * 4,
        out_specs=in_vmem(),
    )(
        held,
        pltpu.with_memory_space_constraint(later_gates, pltpu.VMEM),
        pltpu.with_memory_space_constraint(lane_gate, pltpu.VMEM),
        pltpu.with_memory_space_constraint(ready_gates, pltpu.VMEM),
    )
    home = exchange(back).reshape(16, 2, 8, 8, LANES)
    ordered = pl.pallas_call(
        last_kernel,
        out_shape=jax.ShapeDtypeStruct((16, 8, 2, 8, LANES), jnp.float32),
        in_specs=[in_vmem()],
        out_specs=anywhere(),
        scratch_shapes=[pltpu.SemaphoreType.DMA((8,))],
    )(pltpu.with_memory_space_constraint(home, pltpu.VMEM))
    return ordered.reshape(row_count, 2, LANES).transpose(1, 0, 2).reshape(2, local_amps)


def solution(mesh):
    wide, narrow = mesh.devices.shape
    names = ("top", "rest") + NARROW_BITS
    split_mesh = Mesh(mesh.devices.reshape(2, wide // 2, *([2] * (narrow.bit_length() - 1))), names)
    amplitudes = P(None, names)
    return jax.shard_map(
        local, mesh=split_mesh, in_specs=(amplitudes, P(), P()), out_specs=amplitudes, check_vma=False
    )
```
